128 devices in a mesh: shard: 32 (over y, z_hi, x), tensor: 4 (over z_lo, core).
Axes of the slice: x: 4, y: 4, z: 4 (z_hi: 2, z_lo: 2; z = z_hi * 2 + z_lo), core: 2. Of those that a mesh axis runs over, the one named last changes fastest.
Arguments:
- acts: bfloat16 [32768, 768], P('shard', 'tensor')
- out_grads: bfloat16 [2, 32768, 768], P(None, 'shard', 'tensor')
- sampled_rows: int32 [2, 262144], P(None, 'shard'), may hold values from 0 to 1023
- proj_grad: float32 [768, 768], P(('shard', 'tensor')), may hold values from -600 to 600
- proj_momentum: float32 [768, 768], P(('shard', 'tensor')), may hold values from -6 to 6
- embed_grad: float32 [49152, 768], P(('shard', 'tensor')), may hold values from -36 to 36
- embed_momentum: float32 [49152, 768], P(('shard', 'tensor')), may hold values from -6 to 6
- token_counts: int32 [49152], P(('shard', 'tensor')), may hold values from 0 to 99
Outputs:
- proj_momentum_new: float32 [768, 768], P(('shard', 'tensor'))
- embed_momentum_new: float32 [49152, 768], P(('shard', 'tensor'))
The draws below stay inside these ranges and needn't reach their ends.
Inputs may be any that keep to these rules, and one draw needn't show every extreme that they name: `sampled_rows`: entry j of a row picks token (j // 8192) * 1024 + value, one of the 1024 tokens of its index of shard; repeats are allowed.
All inputs are finite; a program needn't handle non-finite values.
Results may differ from the reference program's by a relative error of at most 0.0003.
Values may be sent and summed in bfloat16 or wider, within the bound.
No kernel may reach another device: no remote copies, remote signals or barrier semaphores. Data moves between devices by JAX's collectives and lax.ppermute only.
A program may use at most 128 MiB of HBM per device.

```python
import math
import jax
import jax.numpy as jnp
from jax import lax

D = 768
VOCAB = 49152
TOK_DEV = 1024
SAMPLE = 2048
NS_ITERS = 3
TOKENS = 32768
SAMPLES = 262144
N_SHARD = 32
N_TENSOR = 4


def scaled_features(key, layers, rows, width):
    key_base, key_rows, key_cols = jax.random.split(key, 3)
    base = jax.random.normal(key_base, (layers, rows, width), jnp.float32)
    lowest = 0.3
    uppermost = 3.0
    spread = math.log(uppermost / lowest)
    row_scale = lowest * jnp.exp(spread * jax.random.uniform(key_rows, (layers, rows, 1), jnp.float32))
    col_scale = lowest * jnp.exp(spread * jax.random.uniform(key_cols, (layers, 1, width), jnp.float32))
    rising = jnp.sqrt(1.0 + 2.0 * jnp.arange(rows, dtype=jnp.float32) / rows)[None, :, None]
    return base * row_scale * col_scale * rising


def draw_acts(key, part):
    return scaled_features(jax.random.fold_in(key, 11), 1, TOKENS, D)[0].astype(jnp.bfloat16)


def draw_out_grads(key, part):
    return scaled_features(jax.random.fold_in(key, 23), 2, TOKENS, D).astype(jnp.bfloat16)


def draw_token_counts(key, part):
    places = jnp.arange(VOCAB, dtype=jnp.int32)
    ceiling = 100 - 68 * places // VOCAB
    raw = jax.random.randint(jax.random.fold_in(key, 37), (VOCAB,), 0, 1048576, dtype=jnp.int32)
    counts = raw * ceiling // 1048576
    counts = jnp.where(places == 0, 99, jnp.where(places == VOCAB - 1, 0, counts))
    return counts.astype(jnp.int32)


def plant(drawn, own_key, smallest, largest):
    place = [jax.random.randint(jax.random.fold_in(own_key, axis), (), 0, length) for axis, length in enumerate(drawn.shape)]
    main_axis = drawn.shape.index(max(drawn.shape))
    next_to = place[:main_axis] + [(place[main_axis] + 1) % drawn.shape[main_axis]] + place[main_axis + 1:]
    return drawn.at[tuple(place)].set(smallest).at[tuple(next_to)].set(largest)


def shard_levels(key, extent, shards, smallest, largest):
    def one(position, parts):
        draws = jax.random.uniform(jax.random.fold_in(jax.random.fold_in(key, 6), position), (parts,), jnp.float32, smallest / len(shards), largest / len(shards))
        return jnp.repeat(jnp.exp(draws), extent[position] // parts).reshape((-1,) + (1,) * (len(extent) - position - 1))

    factor_of = one(*shards[0])
    for cut in shards[1:]:
        factor_of = factor_of * one(*cut)
    return factor_of


def normal_values(own_key, extent, deviation, most, pieces=(), kind=jnp.bfloat16):
    factor_of = shard_levels(own_key, extent, pieces, -0.22, 0.18) if pieces else 1.0
    drawn = jax.random.normal(own_key, extent, jnp.float32) * deviation * factor_of
    return jnp.minimum(jnp.maximum(drawn, -most), most).astype(kind)


def setup_inputs(seed: int = 0) -> dict:
    key_of = jax.random.split(jax.random.key(seed), 9)
    acts = draw_acts(jax.random.fold_in(key_of[8], 71), 0)
    out_grads = draw_out_grads(jax.random.fold_in(key_of[8], 71), 0)
    sampled_rows = plant(jax.random.randint(key_of[2], (2, SAMPLES), 0, TOK_DEV), jax.random.fold_in(key_of[2], 1), 0, TOK_DEV - 1).astype(jnp.int32)
    proj_grad = normal_values(key_of[3], (D, D), 100.0, 600.0, ((0, 128),), jnp.float32)
    proj_momentum = normal_values(key_of[4], (D, D), 1.0, 6.0, ((0, 128),), jnp.float32)
    embed_grad = normal_values(key_of[5], (VOCAB, D), 6.0, 36.0, ((0, 128),), jnp.float32)
    embed_momentum = normal_values(key_of[6], (VOCAB, D), 1.0, 6.0, ((0, 128),), jnp.float32)
    token_counts = draw_token_counts(jax.random.fold_in(key_of[8], 71), 0)
    return dict(acts=acts, out_grads=out_grads, sampled_rows=sampled_rows, proj_grad=proj_grad, proj_momentum=proj_momentum, embed_grad=embed_grad, embed_momentum=embed_momentum, token_counts=token_counts)


momentum_decay = 0.9
damping_root = 0.5
count_scale = 64.0
highest = lax.Precision.HIGHEST

def newton_inverse(factor, trace, shift):
    width = factor.shape[0]
    identity = jnp.eye(width, dtype=jnp.float32)
    norm_sq = jnp.sum(factor * factor) + 2.0 * shift * trace + width * shift * shift
    start_scale = 1.0 / jnp.sqrt(norm_sq)
    damped = factor + shift * identity
    iterate = 2.0 * start_scale * identity - start_scale * start_scale * damped
    for iteration in range(NS_ITERS - 1):
        product = jnp.dot(damped, iterate, precision=highest)
        iterate = 2.0 * iterate - jnp.dot(product, iterate, precision=highest)
    return iterate

def reference(acts, out_grads, sampled_rows, proj_grad, proj_momentum, embed_grad, embed_momentum, token_counts):
    devices_all = N_SHARD * N_TENSOR
    sample_total = SAMPLE * devices_all

    def accumulate(device, carry):
        factors, traces = carry
        device = jnp.asarray(device).astype(jnp.int32)
        chosen = lax.dynamic_slice_in_dim(sampled_rows, device * SAMPLE, SAMPLE, 1).astype(jnp.int32)
        offset = (device // N_TENSOR * TOK_DEV).astype(jnp.int32)
        stacked = jnp.stack([acts[offset + chosen[0]], out_grads[0][offset + chosen[0]], out_grads[1][offset + chosen[1]]]).astype(jnp.float32)
        factors = factors + jnp.einsum('fsd,fse->fde', stacked, stacked, precision=highest)
        traces = traces + lax.optimization_barrier(jnp.sum(stacked * stacked, axis=(1, 2)))
        return (factors, traces)
    start = (jnp.zeros((3, D, D), jnp.float32), jnp.zeros((3,), jnp.float32))
    factors, traces = lax.fori_loop(0, devices_all, accumulate, start)
    factors = factors / sample_total
    traces = traces / sample_total
    count_total = jnp.sum(token_counts.astype(jnp.float32))
    ratio = jnp.sqrt(traces[0] / traces[1])
    embed_ratio = jnp.sqrt(count_total / count_scale / VOCAB / (traces[2] / D))
    a_inverse = newton_inverse(factors[0], traces[0], damping_root * ratio)
    g_inverse = newton_inverse(factors[1], traces[1], damping_root / ratio)
    e_inverse = newton_inverse(factors[2], traces[2], damping_root / embed_ratio)
    mixed = jnp.dot(proj_grad, g_inverse, precision=highest)
    update = jnp.dot(a_inverse, mixed, precision=highest)
    row_scale = token_counts.astype(jnp.float32) / count_scale + damping_root * embed_ratio
    embed_update = jnp.dot(embed_grad, e_inverse, precision=highest) / row_scale[:, None]
    return (momentum_decay * proj_momentum + update, momentum_decay * embed_momentum + embed_update)
```

```python
import jax
import jax.numpy as jnp
from jax import lax
from jax.experimental import pallas as pl
from jax.experimental.pallas import tpu as pltpu
from jax.sharding import Mesh, PartitionSpec as P

D = 768
VOCAB = 49152
TOK = 1024
SAMPLES = 262144
BLK = 128
NB = D // BLK
CHIPS = 64
HALF = BLK // 2
STEPS = 7

momentum_decay = 0.9
damping_root = 0.5
count_scale = 64.0

CHIP_AXES = ("y", "zh", "x", "zl")
f32 = jnp.float32
bf16 = jnp.bfloat16

BLOCKS = [(f, i, j) for f in range(3) for i in range(NB) for j in range(i, NB)]


def vmem():
    return pl.BlockSpec(memory_space=pltpu.VMEM)


def smem():
    return pl.BlockSpec(memory_space=pltpu.SMEM)


def params():
    return pltpu.CompilerParams(vmem_limit_bytes=60 * 1024 * 1024)


def nt_dot(a, b):
    return lax.dot_general(a, b, (((1,), (1,)), ((), ())), preferred_element_type=f32)


def nn_dot(a, b):
    return lax.dot_general(a, b, (((1,), (0,)), ((), ())), preferred_element_type=f32)


def split(x):
    hi = x.astype(bf16)
    return hi, (x - hi.astype(f32)).astype(bf16)


def histogram_kernel(info, ids_ref, out_ref):
    first = info[0] * 4
    width = 1024
    high_rows = lax.broadcasted_iota(jnp.int32, (16, width), 0) + first
    low_rows = lax.broadcasted_iota(jnp.int32, (BLK, width), 0)
    for k in range(2):
        total = jnp.zeros((16, BLK), f32)
        for part in range(8):
            ids = ids_ref[k : k + 1, part * width : (part + 1) * width]
            high = (high_rows == (ids >> 7)).astype(f32).astype(bf16)
            low = (low_rows == (ids & 127)).astype(f32).astype(bf16)
            total = total + nt_dot(high, low)
        out_ref[k] = total


def gram_kernel(info, hist_ref, own_ref, own_c_ref, other_ref, other_c_ref, count_ref, out_ref, x_ref):
    zl, core = info[0], info[1]
    places = [2 * zl + core, 2 * zl + 1 - core, 2 * (1 - zl) + core, 2 * (1 - zl) + 1 - core]
    tokens = jnp.sum(count_ref[...].astype(f32), keepdims=True).reshape(1, 1)
    out_ref[CHIPS - 1] = jnp.broadcast_to(tokens, (HALF, BLK)).astype(out_ref.dtype)
    for f in range(3):
        for place, ref in zip(places, (own_ref, own_c_ref, other_ref, other_c_ref)):
            x_ref[pl.ds(pl.multiple_of(place * 192, 192), 192), :] = ref[f]
        x = x_ref[...]
        left = jnp.concatenate(
            [x_ref[pl.ds(pl.multiple_of(i * BLK + core * HALF, HALF), HALF), :] for i in range(NB)], axis=0
        )
        row = 1 if f == 2 else 0
        weight = jnp.concatenate([hist_ref[row, h : h + 1, :] for h in range(4)], axis=1)
        hi, lo = split(left.astype(f32) * weight)
        gram = nt_dot(hi, x) + nt_dot(lo, x)
        for b, (g, i, j) in enumerate(BLOCKS):
            if g == f:
                out_ref[b] = gram[i * HALF : (i + 1) * HALF, j * BLK : (j + 1) * BLK].astype(out_ref.dtype)


def total_kernel(in_ref, out_ref):
    total = jnp.sum(in_ref[...].astype(f32), axis=0) * (1.0 / SAMPLES)
    for s in range(CHIPS):
        out_ref[s] = total.astype(out_ref.dtype)


def step(y, start, hi_ref, lo_ref):
    y_hi, y_lo = split(y)
    hi, lo = hi_ref[...], lo_ref[...]
    return start + y - (nn_dot(y_hi, hi) + nn_dot(y_lo, hi) + nn_dot(y_hi, lo))


def finish_kernel(
    info, own_ref, other_ref, p_ref, p_mom_ref, g_ref, e_mom_ref, count_ref,
    p_out_ref, e_out_ref, full_ref, hi_ref, lo_ref, y_ref,
):
    core, flat = info[0], info[1]
    rows = lax.broadcasted_iota(jnp.int32, (BLK, BLK), 0)
    cols = lax.broadcasted_iota(jnp.int32, (BLK, BLK), 1)
    diagonal = rows == cols
    zero = jnp.zeros((BLK, BLK), f32)
    squares = [zero, zero, zero]
    traces = [zero, zero, zero]
    for b, (f, i, j) in enumerate(BLOCKS):
        for part, ref in ((core, own_ref), (1 - core, other_ref)):
            start = pl.multiple_of(i * BLK + part * HALF, HALF)
            full_ref[f, pl.ds(start, HALF), j * BLK : (j + 1) * BLK] = ref[b].astype(f32)
        block = full_ref[f, i * BLK : (i + 1) * BLK, j * BLK : (j + 1) * BLK]
        if i == j:
            squares[f] = squares[f] + block * block
            traces[f] = traces[f] + jnp.where(diagonal, block, 0.0)
        else:
            squares[f] = squares[f] + 2.0 * block * block
    squares = [jnp.sum(s, keepdims=True) for s in squares]
    traces = [jnp.sum(t, keepdims=True) for t in traces]
    tokens = (own_ref[CHIPS - 1][0:1, 0:1] + other_ref[CHIPS - 1][0:1, 0:1]) * float(SAMPLES)
    ratio = jnp.sqrt(traces[0] / traces[1])
    embed_ratio = jnp.sqrt(tokens / count_scale / VOCAB / (traces[2] / D))
    shifts = [damping_root * ratio, damping_root / ratio, damping_root / embed_ratio]
    scales = []
    for f in range(3):
        q = squares[f] + 2.0 * shifts[f] * traces[f] + D * shifts[f] * shifts[f]
        scales.append(1.0 / jnp.sqrt(q))
    for b, (f, i, j) in enumerate(BLOCKS):
        block = full_ref[f, i * BLK : (i + 1) * BLK, j * BLK : (j + 1) * BLK]
        if i == j:
            block = block + jnp.where(diagonal, shifts[f], 0.0)
        block = block * scales[f]
        hi, lo = split(block)
        hi_ref[f, i * BLK : (i + 1) * BLK, j * BLK : (j + 1) * BLK] = hi
        lo_ref[f, i * BLK : (i + 1) * BLK, j * BLK : (j + 1) * BLK] = lo
        if i != j:
            hi, lo = split(block.T)
            hi_ref[f, j * BLK : (j + 1) * BLK, i * BLK : (i + 1) * BLK] = hi
            lo_ref[f, j * BLK : (j + 1) * BLK, i * BLK : (i + 1) * BLK] = lo

    half = 192
    row = lax.broadcasted_iota(jnp.int32, (8, D), 0)
    col = lax.broadcasted_iota(jnp.int32, (8, D), 1)
    unit = jnp.where((row < 6) & (col == flat * 6 + row), 1.0, 0.0)

    def first(_, carry):
        a, y = carry
        a = step(a, unit, hi_ref.at[0], lo_ref.at[0])
        y = step(y, g_ref[0:half, :], hi_ref.at[2], lo_ref.at[2])
        return a, y

    a, y = lax.fori_loop(0, STEPS, first, (unit, g_ref[0:half, :]))
    y_ref[0:half, :] = y
    a_hi, a_lo = split(a * scales[0])
    p_hi, p_lo = split(p_ref[...])
    mixed = nn_dot(a_hi, p_hi) + nn_dot(a_lo, p_hi) + nn_dot(a_hi, p_lo)

    def second(_, carry):
        a, y = carry
        a = step(a, mixed, hi_ref.at[1], lo_ref.at[1])
        y = step(y, g_ref[half:, :], hi_ref.at[2], lo_ref.at[2])
        return a, y

    a, y = lax.fori_loop(0, STEPS, second, (mixed, g_ref[half:, :]))
    y_ref[half:, :] = y
    p_out_ref[...] = momentum_decay * p_mom_ref[...] + (a * scales[1])[0:6]
    row_scale = count_ref[...].astype(f32) / count_scale + damping_root * embed_ratio
    e_out_ref[...] = momentum_decay * e_mom_ref[...] + y_ref[...] * scales[2] / row_scale


def to_other(x, axis):
    return lax.ppermute(x, axis, [(0, 1), (1, 0)])


def exchange(x):
    return lax.all_to_all(x, CHIP_AXES, split_axis=0, concat_axis=0, tiled=True)


def per_device(acts, out_grads, sampled_rows, proj_grad, proj_momentum, embed_grad, embed_momentum, token_counts):
    zl, core = lax.axis_index("zl"), lax.axis_index("c")
    chip = lax.axis_index(CHIP_AXES)
    flat = chip * 2 + core

    features = jnp.concatenate([acts.T[None], jnp.transpose(out_grads, (0, 2, 1))], axis=0)
    keep = lax.dynamic_slice_in_dim(features, zl * 512, 512, 2)
    send = lax.dynamic_slice_in_dim(features, (1 - zl) * 512, 512, 2)
    other = to_other(send, "zl")
    keep_c = to_other(keep, "c")
    other_c = to_other(other, "c")

    hist = pl.pallas_call(
        histogram_kernel,
        out_shape=jax.ShapeDtypeStruct((2, 16, BLK), f32),
        in_specs=[smem(), vmem()],
        out_specs=vmem(),
        compiler_params=params(),
        name="histogram",
    )(jnp.stack([zl]), sampled_rows)

    parts = pl.pallas_call(
        gram_kernel,
        out_shape=jax.ShapeDtypeStruct((CHIPS, HALF, BLK), f32),
        in_specs=[smem()] + [vmem()] * 6,
        out_specs=vmem(),
        scratch_shapes=[pltpu.VMEM((D, 512), bf16)],
        compiler_params=params(),
        name="gram",
    )(jnp.stack([zl, core]), hist, keep, keep_c, other, other_c, token_counts.reshape(3, BLK))

    rows = proj_grad.shape[0]
    p_own = exchange(jnp.broadcast_to(proj_grad[None], (CHIPS,) + proj_grad.shape))
    p_other = to_other(p_own, "c")
    p_pair = jnp.stack([jnp.where(core == 0, p_own, p_other), jnp.where(core == 0, p_other, p_own)], axis=1)
    p_full = p_pair.reshape(D, D)

    arrived = exchange(parts)
    spread = pl.pallas_call(
        total_kernel,
        out_shape=jax.ShapeDtypeStruct((CHIPS, HALF, BLK), f32),
        in_specs=[vmem()],
        out_specs=vmem(),
        compiler_params=params(),
        name="total",
    )(arrived)
    own_blocks = exchange(spread)
    other_blocks = to_other(own_blocks, "c")

    return pl.pallas_call(
        finish_kernel,
        out_shape=(
            jax.ShapeDtypeStruct(proj_momentum.shape, f32),
            jax.ShapeDtypeStruct(embed_momentum.shape, f32),
        ),
        in_specs=[smem()] + [vmem()] * 7,
        out_specs=(vmem(), vmem()),
        scratch_shapes=[
            pltpu.VMEM((3, D, D), f32),
            pltpu.VMEM((3, D, D), bf16),
            pltpu.VMEM((3, D, D), bf16),
            pltpu.VMEM((384, D), f32),
        ],
        compiler_params=params(),
        name="finish",
    )(
        jnp.stack([core, flat]), own_blocks, other_blocks, p_full, proj_momentum, embed_grad, embed_momentum,
        token_counts.reshape(-1, 1),
    )


def solution(mesh):
    fine = Mesh(mesh.devices.reshape(4, 2, 4, 2, 2), ("y", "zh", "x", "zl", "c"))
    shard, tensor = ("y", "zh", "x"), ("zl", "c")
    rows = P(shard + tensor, None)
    return jax.shard_map(
        per_device,
        mesh=fine,
        in_specs=(
            P(shard, tensor), P(None, shard, tensor), P(None, shard),
            rows, rows, rows, rows, P(shard + tensor),
        ),
        out_specs=(rows, rows),
        check_vma=False,
    )
```

```python
import jax
import jax.numpy as jnp
from jax import lax
from jax.experimental import pallas as pl
from jax.experimental.pallas import tpu as pltpu
from jax.sharding import Mesh, PartitionSpec as P

D = 768
VOCAB = 49152
TOK = 1024
SAMPLES = 262144
BLK = 128
NB = D // BLK
CHIPS = 64
HALF = BLK // 2
STEPS = 7

momentum_decay = 0.9
damping_root = 0.5
count_scale = 64.0

CHIP_AXES = ("y", "zh", "x", "zl")
f32 = jnp.float32
bf16 = jnp.bfloat16

BLOCKS = [(f, i, j) for f in range(3) for i in range(NB) for j in range(i, NB)]


def vmem():
    return pl.BlockSpec(memory_space=pltpu.VMEM)


def smem():
    return pl.BlockSpec(memory_space=pltpu.SMEM)


def params():
    return pltpu.CompilerParams(vmem_limit_bytes=60 * 1024 * 1024)


def nt_dot(a, b):
    return lax.dot_general(a, b, (((1,), (1,)), ((), ())), preferred_element_type=f32)


def nn_dot(a, b):
    return lax.dot_general(a, b, (((1,), (0,)), ((), ())), preferred_element_type=f32)


def split(x):
    hi = x.astype(bf16)
    return hi, (x - hi.astype(f32)).astype(bf16)


def histogram_kernel(info, ids_ref, out_ref):
    first = info[0] * 4
    width = 1024
    high_rows = lax.broadcasted_iota(jnp.int32, (16, width), 0) + first
    low_rows = lax.broadcasted_iota(jnp.int32, (BLK, width), 0)
    for k in range(2):
        total = jnp.zeros((16, BLK), f32)
        for part in range(8):
            ids = ids_ref[k : k + 1, part * width : (part + 1) * width]
            high = (high_rows == (ids >> 7)).astype(f32).astype(bf16)
            low = (low_rows == (ids & 127)).astype(f32).astype(bf16)
            total = total + nt_dot(high, low)
        out_ref[k] = total


def swap_halves(x):
    return pltpu.roll(x, HALF, 1)


def pair_up(x, lane):
    hi, lo = split(x)
    return jnp.where(lane < HALF, hi.astype(f32), lo.astype(f32))


def gram_kernel(info, hist_ref, own_ref, own_c_ref, other_ref, other_c_ref, count_ref, out_ref, x_ref):
    zl, core = info[0], info[1]
    places = [2 * zl + core, 2 * zl + 1 - core, 2 * (1 - zl) + core, 2 * (1 - zl) + 1 - core]
    on_diagonal = (
        lax.broadcasted_iota(jnp.int32, (HALF, BLK), 1)
        == lax.broadcasted_iota(jnp.int32, (HALF, BLK), 0) + core * HALF
    )
    exact = []
    for f in range(3):
        for place, ref in zip(places, (own_ref, own_c_ref, other_ref, other_c_ref)):
            x_ref[pl.ds(pl.multiple_of(place * 192, 192), 192), :] = ref[f]
        x = x_ref[...]
        left = jnp.concatenate(
            [x_ref[pl.ds(pl.multiple_of(i * BLK + core * HALF, HALF), HALF), :] for i in range(NB)], axis=0
        )
        row = 1 if f == 2 else 0
        weight = jnp.concatenate([hist_ref[row, h : h + 1, :] for h in range(4)], axis=1)
        hi, lo = split(left.astype(f32) * weight)
        gram = nt_dot(hi, x) + nt_dot(lo, x)
        for b, (g, i, j) in enumerate(BLOCKS):
            if g == f:
                block = gram[i * HALF : (i + 1) * HALF, j * BLK : (j + 1) * BLK]
                out_ref[b] = block.astype(bf16)
                if i == j:
                    exact.append(jnp.sum(jnp.where(on_diagonal, block, 0.0), axis=0, keepdims=True))
    tokens = jnp.sum(count_ref[...].astype(f32), keepdims=True).reshape(1, 1)
    lane = lax.broadcasted_iota(jnp.int32, (1, BLK), 1)
    exact.append(jnp.where(lane < HALF, tokens, 0.0))
    exact = jnp.concatenate(exact + [jnp.zeros((HALF - len(exact), BLK), f32)], axis=0)
    exact = exact + swap_halves(exact)
    lane = lax.broadcasted_iota(jnp.int32, (HALF, BLK), 1)
    out_ref[CHIPS - 1] = pair_up(exact, lane).astype(bf16)


def total_kernel(info, in_ref, out_ref):
    total = jnp.sum(in_ref[...].astype(f32), axis=0) * (1.0 / SAMPLES)
    lane = lax.broadcasted_iota(jnp.int32, (HALF, BLK), 1)
    exact = pair_up(total + swap_halves(total), lane)
    total = jnp.where(info[0] == CHIPS - 1, exact, total).astype(bf16)
    for s in range(CHIPS):
        out_ref[s] = total


def step(y, start, keep, scale, r_ref):
    hi, lo = split(y)
    return start + y * keep - scale * (nn_dot(hi, r_ref[...]) + nn_dot(lo, r_ref[...]))


def thin_step(y, start, keep, scale, r_ref):
    hi, lo = split(y)
    both = nn_dot(jnp.concatenate([hi, lo], axis=0), r_ref[...])
    return start + y * keep - scale * (both[:8] + both[8:])


def finish_kernel(
    info, own_ref, other_ref, p_ref, p_mom_ref, g_ref, e_mom_ref, count_ref,
    p_out_ref, e_out_ref, r_ref, y_ref,
):
    core, flat = info[0], info[1]
    row = lax.broadcasted_iota(jnp.int32, (HALF, BLK), 0)
    col = lax.broadcasted_iota(jnp.int32, (HALF, BLK), 1)
    squares = [jnp.zeros((HALF, BLK), f32) for _ in range(3)]
    for part, ref in ((core, own_ref), (1 - core, other_ref)):
        off_diagonal = col != row + part * HALF
        for b, (f, i, j) in enumerate(BLOCKS):
            start = pl.multiple_of(i * BLK + part * HALF, HALF)
            block = ref[b]
            wide = block.astype(f32)
            if i == j:
                wide = jnp.where(off_diagonal, wide, 0.0)
                block = wide.astype(bf16)
                squares[f] = squares[f] + wide * wide
            else:
                squares[f] = squares[f] + 2.0 * (wide * wide)
            r_ref[f, pl.ds(start, HALF), j * BLK : (j + 1) * BLK] = block
    for b, (f, i, j) in enumerate(BLOCKS):
        if i != j:
            block = r_ref[f, i * BLK : (i + 1) * BLK, j * BLK : (j + 1) * BLK]
            r_ref[f, j * BLK : (j + 1) * BLK, i * BLK : (i + 1) * BLK] = block.T

    own = own_ref[CHIPS - 1].astype(f32)
    other = other_ref[CHIPS - 1].astype(f32)
    own = own + swap_halves(own)
    other = other + swap_halves(other)
    exact = jnp.where((col < HALF) == (core == 0), own, other)
    tokens = (own + other)[18:19, 0:1] * float(SAMPLES)
    diagonals = [
        jnp.concatenate([exact[f * NB + i : f * NB + i + 1, :] for i in range(NB)], axis=1) for f in range(3)
    ]
    traces = [jnp.sum(d, keepdims=True) for d in diagonals]
    squares = [jnp.sum(s, keepdims=True) + jnp.sum(d * d, keepdims=True) for s, d in zip(squares, diagonals)]
    ratio = jnp.sqrt(traces[0] / traces[1])
    embed_ratio = jnp.sqrt(tokens / count_scale / VOCAB / (traces[2] / D))
    shifts = [damping_root * ratio, damping_root / ratio, damping_root / embed_ratio]
    scales, keeps = [], []
    for f in range(3):
        q = squares[f] + 2.0 * shifts[f] * traces[f] + D * shifts[f] * shifts[f]
        scales.append(1.0 / jnp.sqrt(q))
        keeps.append(1.0 - scales[f] * (diagonals[f] + shifts[f]))

    half = 192
    row = lax.broadcasted_iota(jnp.int32, (8, D), 0)
    col = lax.broadcasted_iota(jnp.int32, (8, D), 1)
    unit = jnp.where((row < 6) & (col == flat * 6 + row), 1.0, 0.0)

    def first(_, carry):
        a, y = carry
        a = thin_step(a, unit, keeps[0], scales[0], r_ref.at[0])
        y = step(y, g_ref[0:half, :], keeps[2], scales[2], r_ref.at[2])
        return a, y

    a, y = lax.fori_loop(0, STEPS, first, (unit, g_ref[0:half, :]))
    y_ref[0:half, :] = y
    a_hi, a_lo = split(a * scales[0])
    p_hi, p_lo = split(p_ref[...])
    mixed = nn_dot(a_hi, p_hi) + nn_dot(a_lo, p_hi) + nn_dot(a_hi, p_lo)

    def second(_, carry):
        a, y = carry
        a = thin_step(a, mixed, keeps[1], scales[1], r_ref.at[1])
        y = step(y, g_ref[half:, :], keeps[2], scales[2], r_ref.at[2])
        return a, y

    a, y = lax.fori_loop(0, STEPS, second, (mixed, g_ref[half:, :]))
    y_ref[half:, :] = y
    p_out_ref[...] = momentum_decay * p_mom_ref[...] + (a * scales[1])[0:6]
    row_scale = count_ref[...].astype(f32) / count_scale + damping_root * embed_ratio
    e_out_ref[...] = momentum_decay * e_mom_ref[...] + y_ref[...] * scales[2] / row_scale


def to_other(x, axis):
    return lax.ppermute(x, axis, [(0, 1), (1, 0)])


def exchange(x):
    return lax.all_to_all(x, CHIP_AXES, split_axis=0, concat_axis=0, tiled=True)


def per_device(acts, out_grads, sampled_rows, proj_grad, proj_momentum, embed_grad, embed_momentum, token_counts):
    zl, core = lax.axis_index("zl"), lax.axis_index("c")
    chip = lax.axis_index(CHIP_AXES)
    flat = chip * 2 + core

    features = jnp.concatenate([acts.T[None], jnp.transpose(out_grads, (0, 2, 1))], axis=0)
    keep = lax.dynamic_slice_in_dim(features, zl * 512, 512, 2)
    send = lax.dynamic_slice_in_dim(features, (1 - zl) * 512, 512, 2)
    other = to_other(send, "zl")
    keep_c = to_other(keep, "c")
    other_c = to_other(other, "c")

    hist = pl.pallas_call(
        histogram_kernel,
        out_shape=jax.ShapeDtypeStruct((2, 16, BLK), f32),
        in_specs=[smem(), vmem()],
        out_specs=vmem(),
        compiler_params=params(),
        name="histogram",
    )(jnp.stack([zl]), sampled_rows)

    parts = pl.pallas_call(
        gram_kernel,
        out_shape=jax.ShapeDtypeStruct((CHIPS, HALF, BLK), bf16),
        in_specs=[smem()] + [vmem()] * 6,
        out_specs=vmem(),
        scratch_shapes=[pltpu.VMEM((D, 512), bf16)],
        compiler_params=params(),
        name="gram",
    )(jnp.stack([zl, core]), hist, keep, keep_c, other, other_c, token_counts.reshape(3, BLK))

    p_own = exchange(jnp.broadcast_to(proj_grad[None], (CHIPS,) + proj_grad.shape))
    p_other = to_other(p_own, "c")
    parts, p_own, p_other = lax.optimization_barrier((parts, p_own, p_other))
    arrived = exchange(parts)
    p_pair = jnp.stack([jnp.where(core == 0, p_own, p_other), jnp.where(core == 0, p_other, p_own)], axis=1)
    p_full = p_pair.reshape(D, D)

    spread = pl.pallas_call(
        total_kernel,
        out_shape=jax.ShapeDtypeStruct((CHIPS, HALF, BLK), bf16),
        in_specs=[smem(), vmem()],
        out_specs=vmem(),
        compiler_params=params(),
        name="total",
    )(jnp.stack([chip]), arrived)
    own_blocks = exchange(spread)
    other_blocks = to_other(own_blocks, "c")

    return pl.pallas_call(
        finish_kernel,
        out_shape=(
            jax.ShapeDtypeStruct(proj_momentum.shape, f32),
            jax.ShapeDtypeStruct(embed_momentum.shape, f32),
        ),
        in_specs=[smem()] + [vmem()] * 7,
        out_specs=(vmem(), vmem()),
        scratch_shapes=[
            pltpu.VMEM((3, D, D), bf16),
            pltpu.VMEM((384, D), f32),
        ],
        compiler_params=params(),
        name="finish",
    )(
        jnp.stack([core, flat]), own_blocks, other_blocks, p_full, proj_momentum, embed_grad, embed_momentum,
        token_counts.reshape(-1, 1),
    )


def solution(mesh):
    fine = Mesh(mesh.devices.reshape(4, 2, 4, 2, 2), ("y", "zh", "x", "zl", "c"))
    shard, tensor = ("y", "zh", "x"), ("zl", "c")
    rows = P(shard + tensor, None)
    return jax.shard_map(
        per_device,
        mesh=fine,
        in_specs=(
            P(shard, tensor), P(None, shard, tensor), P(None, shard),
            rows, rows, rows, rows, P(shard + tensor),
        ),
        out_specs=(rows, rows),
        check_vma=False,
    )
```

```python
import jax
import jax.numpy as jnp
from jax import lax
from jax.experimental import pallas as pl
from jax.experimental.pallas import tpu as pltpu
from jax.sharding import Mesh, PartitionSpec as P

D = 768
VOCAB = 49152
TOK = 1024
SAMPLES = 262144
BLK = 128
NB = D // BLK
CHIPS = 64
HALF = BLK // 2
STEPS = 7

momentum_decay = 0.9
damping_root = 0.5
count_scale = 64.0

CHIP_AXES = ("y", "zh", "x", "zl")
f32 = jnp.float32
bf16 = jnp.bfloat16

BLOCKS = [(f, i, j) for f in range(3) for i in range(NB) for j in range(i, NB)]


def vmem():
    return pl.BlockSpec(memory_space=pltpu.VMEM)


def smem():
    return pl.BlockSpec(memory_space=pltpu.SMEM)


def params():
    return pltpu.CompilerParams(vmem_limit_bytes=60 * 1024 * 1024)


def nt_dot(a, b):
    return lax.dot_general(a, b, (((1,), (1,)), ((), ())), preferred_element_type=f32)


def nn_dot(a, b):
    return lax.dot_general(a, b, (((1,), (0,)), ((), ())), preferred_element_type=f32)


def split(x):
    hi = x.astype(bf16)
    return hi, (x - hi.astype(f32)).astype(bf16)


def histogram_kernel(info, ids_ref, out_ref):
    first = info[0] * 4
    width = 1024
    high_rows = lax.broadcasted_iota(jnp.int32, (16, width), 0) + first
    low_rows = lax.broadcasted_iota(jnp.int32, (BLK, width), 0)
    for k in range(2):
        total = jnp.zeros((16, BLK), f32)
        for part in range(8):
            ids = ids_ref[k : k + 1, part * width : (part + 1) * width]
            high = (high_rows == (ids >> 7)).astype(f32).astype(bf16)
            low = (low_rows == (ids & 127)).astype(f32).astype(bf16)
            total = total + nt_dot(high, low)
        out_ref[k] = total


def swap_halves(x):
    return pltpu.roll(x, HALF, 1)


def pair_up(x, lane):
    hi, lo = split(x)
    return jnp.where(lane < HALF, hi.astype(f32), lo.astype(f32))


def gram_kernel(info, hist_ref, own_ref, own_c_ref, other_ref, other_c_ref, count_ref, out_ref, x_ref):
    zl, core = info[0], info[1]
    places = [2 * zl + core, 2 * zl + 1 - core, 2 * (1 - zl) + core, 2 * (1 - zl) + 1 - core]
    on_diagonal = (
        lax.broadcasted_iota(jnp.int32, (HALF, BLK), 1)
        == lax.broadcasted_iota(jnp.int32, (HALF, BLK), 0) + core * HALF
    )
    exact = []
    for f in range(3):
        for place, ref in zip(places, (own_ref, own_c_ref, other_ref, other_c_ref)):
            x_ref[pl.ds(pl.multiple_of(place * 192, 192), 192), :] = ref[f]
        x = x_ref[...]
        left = jnp.concatenate(
            [x_ref[pl.ds(pl.multiple_of(i * BLK + core * HALF, HALF), HALF), :] for i in range(NB)], axis=0
        )
        row = 1 if f == 2 else 0
        weight = jnp.concatenate([hist_ref[row, h : h + 1, :] for h in range(4)], axis=1)
        hi, lo = split(left.astype(f32) * weight)
        gram = nt_dot(hi, x) + nt_dot(lo, x)
        for b, (g, i, j) in enumerate(BLOCKS):
            if g == f:
                block = gram[i * HALF : (i + 1) * HALF, j * BLK : (j + 1) * BLK]
                out_ref[b] = block.astype(bf16)
                if i == j:
                    exact.append(jnp.sum(jnp.where(on_diagonal, block, 0.0), axis=0, keepdims=True))
    tokens = jnp.sum(count_ref[...].astype(f32), keepdims=True).reshape(1, 1)
    lane = lax.broadcasted_iota(jnp.int32, (1, BLK), 1)
    exact.append(jnp.where(lane < HALF, tokens, 0.0))
    exact = jnp.concatenate(exact + [jnp.zeros((HALF - len(exact), BLK), f32)], axis=0)
    exact = exact + swap_halves(exact)
    lane = lax.broadcasted_iota(jnp.int32, (HALF, BLK), 1)
    out_ref[CHIPS - 1] = pair_up(exact, lane).astype(bf16)


def total_kernel(info, in_ref, out_ref):
    total = jnp.sum(in_ref[...].astype(f32), axis=0) * (1.0 / SAMPLES)
    lane = lax.broadcasted_iota(jnp.int32, (HALF, BLK), 1)
    exact = pair_up(total + swap_halves(total), lane)
    total = jnp.where(info[0] == CHIPS - 1, exact, total).astype(bf16)
    for s in range(CHIPS):
        out_ref[s] = total


def step(y, start, keep, scale, r_ref):
    hi, lo = split(y)
    return start + y * keep - scale * (nn_dot(hi, r_ref[...]) + nn_dot(lo, r_ref[...]))


def thin_step(y, start, keep, scale, r_ref):
    hi, lo = split(y)
    both = nn_dot(jnp.concatenate([hi, lo], axis=0), r_ref[...])
    return start + y * keep - scale * (both[:8] + both[8:])


def finish_kernel(
    info, own_ref, other_ref, p_ref, p_mom_ref, g_ref, e_mom_ref, count_ref,
    p_out_ref, e_out_ref, r_ref, y_ref,
):
    core, flat = info[0], info[1]
    row = lax.broadcasted_iota(jnp.int32, (HALF, BLK), 0)
    col = lax.broadcasted_iota(jnp.int32, (HALF, BLK), 1)
    squares = [jnp.zeros((HALF, BLK), f32) for _ in range(3)]
    for part, ref in ((core, own_ref), (1 - core, other_ref)):
        off_diagonal = col != row + part * HALF
        for b, (f, i, j) in enumerate(BLOCKS):
            start = pl.multiple_of(i * BLK + part * HALF, HALF)
            block = ref[b]
            wide = block.astype(f32)
            if i == j:
                wide = jnp.where(off_diagonal, wide, 0.0)
                block = wide.astype(bf16)
                squares[f] = squares[f] + wide * wide
            else:
                squares[f] = squares[f] + 2.0 * (wide * wide)
            r_ref[f, pl.ds(start, HALF), j * BLK : (j + 1) * BLK] = block
    for b, (f, i, j) in enumerate(BLOCKS):
        if i != j:
            block = r_ref[f, i * BLK : (i + 1) * BLK, j * BLK : (j + 1) * BLK]
            r_ref[f, j * BLK : (j + 1) * BLK, i * BLK : (i + 1) * BLK] = block.T

    own = own_ref[CHIPS - 1].astype(f32)
    other = other_ref[CHIPS - 1].astype(f32)
    own = own + swap_halves(own)
    other = other + swap_halves(other)
    exact = jnp.where((col < HALF) == (core == 0), own, other)
    tokens = (own + other)[18:19, 0:1] * float(SAMPLES)
    diagonals = [
        jnp.concatenate([exact[f * NB + i : f * NB + i + 1, :] for i in range(NB)], axis=1) for f in range(3)
    ]
    traces = [jnp.sum(d, keepdims=True) for d in diagonals]
    squares = [jnp.sum(s, keepdims=True) + jnp.sum(d * d, keepdims=True) for s, d in zip(squares, diagonals)]
    ratio = jnp.sqrt(traces[0] / traces[1])
    embed_ratio = jnp.sqrt(tokens / count_scale / VOCAB / (traces[2] / D))
    shifts = [damping_root * ratio, damping_root / ratio, damping_root / embed_ratio]
    scales, keeps = [], []
    for f in range(3):
        q = squares[f] + 2.0 * shifts[f] * traces[f] + D * shifts[f] * shifts[f]
        scales.append(1.0 / jnp.sqrt(q))
        keeps.append(1.0 - scales[f] * (diagonals[f] + shifts[f]))

    half = 192
    row = lax.broadcasted_iota(jnp.int32, (8, D), 0)
    col = lax.broadcasted_iota(jnp.int32, (8, D), 1)
    unit = jnp.where((row < 6) & (col == flat * 6 + row), 1.0, 0.0)

    def first(_, carry):
        a, y = carry
        a = thin_step(a, unit, keeps[0], scales[0], r_ref.at[0])
        y = step(y, g_ref[0:half, :], keeps[2], scales[2], r_ref.at[2])
        return a, y

    a, y = lax.fori_loop(0, STEPS, first, (unit, g_ref[0:half, :]))
    y_ref[0:half, :] = y
    a_hi, a_lo = split(a * scales[0])
    p_hi, p_lo = split(p_ref[...])
    mixed = nn_dot(a_hi, p_hi) + nn_dot(a_lo, p_hi) + nn_dot(a_hi, p_lo)

    def second(_, carry):
        a, y = carry
        a = thin_step(a, mixed, keeps[1], scales[1], r_ref.at[1])
        y = step(y, g_ref[half:, :], keeps[2], scales[2], r_ref.at[2])
        return a, y

    a, y = lax.fori_loop(0, STEPS, second, (mixed, g_ref[half:, :]))
    y_ref[half:, :] = y
    p_out_ref[...] = momentum_decay * p_mom_ref[...] + (a * scales[1])[0:6]
    row_scale = count_ref[...].astype(f32) / count_scale + damping_root * embed_ratio
    e_out_ref[...] = momentum_decay * e_mom_ref[...] + y_ref[...] * scales[2] / row_scale


def to_other(x, axis):
    return lax.ppermute(x, axis, [(0, 1), (1, 0)])


def exchange(x):
    return lax.all_to_all(x, CHIP_AXES, split_axis=0, concat_axis=0, tiled=True)


def per_device(acts, out_grads, sampled_rows, proj_grad, proj_momentum, embed_grad, embed_momentum, token_counts):
    zl, core = lax.axis_index("zl"), lax.axis_index("c")
    chip = lax.axis_index(CHIP_AXES)
    flat = chip * 2 + core

    features = jnp.concatenate([acts.T[None], jnp.transpose(out_grads, (0, 2, 1))], axis=0)
    keep = lax.dynamic_slice_in_dim(features, zl * 512, 512, 2)
    send = lax.dynamic_slice_in_dim(features, (1 - zl) * 512, 512, 2)
    send, keep, p_rows = lax.optimization_barrier((send, keep, proj_grad))
    other = to_other(send, "zl")
    keep_c = to_other(keep, "c")
    other_c = to_other(other, "c")

    hist = pl.pallas_call(
        histogram_kernel,
        out_shape=jax.ShapeDtypeStruct((2, 16, BLK), f32),
        in_specs=[smem(), vmem()],
        out_specs=vmem(),
        compiler_params=params(),
        name="histogram",
    )(jnp.stack([zl]), sampled_rows)

    parts = pl.pallas_call(
        gram_kernel,
        out_shape=jax.ShapeDtypeStruct((CHIPS, HALF, BLK), bf16),
        in_specs=[smem()] + [vmem()] * 6,
        out_specs=vmem(),
        scratch_shapes=[pltpu.VMEM((D, 512), bf16)],
        compiler_params=params(),
        name="gram",
    )(jnp.stack([zl, core]), hist, keep, keep_c, other, other_c, token_counts.reshape(3, BLK))

    p_own = exchange(jnp.broadcast_to(p_rows[None], (CHIPS,) + proj_grad.shape))
    parts, p_own = lax.optimization_barrier((parts, p_own))
    arrived = exchange(parts)
    p_other = to_other(p_own, "c")
    p_pair = jnp.stack([jnp.where(core == 0, p_own, p_other), jnp.where(core == 0, p_other, p_own)], axis=1)
    p_full = p_pair.reshape(D, D)

    spread = pl.pallas_call(
        total_kernel,
        out_shape=jax.ShapeDtypeStruct((CHIPS, HALF, BLK), bf16),
        in_specs=[smem(), vmem()],
        out_specs=vmem(),
        compiler_params=params(),
        name="total",
    )(jnp.stack([chip]), arrived)
    own_blocks = exchange(spread)
    other_blocks = to_other(own_blocks, "c")

    return pl.pallas_call(
        finish_kernel,
        out_shape=(
            jax.ShapeDtypeStruct(proj_momentum.shape, f32),
            jax.ShapeDtypeStruct(embed_momentum.shape, f32),
        ),
        in_specs=[smem()] + [vmem()] * 7,
        out_specs=(vmem(), vmem()),
        scratch_shapes=[
            pltpu.VMEM((3, D, D), bf16),
            pltpu.VMEM((384, D), f32),
        ],
        compiler_params=params(),
        name="finish",
    )(
        jnp.stack([core, flat]), own_blocks, other_blocks, p_full, proj_momentum, embed_grad, embed_momentum,
        token_counts.reshape(-1, 1),
    )


def solution(mesh):
    fine = Mesh(mesh.devices.reshape(4, 2, 4, 2, 2), ("y", "zh", "x", "zl", "c"))
    shard, tensor = ("y", "zh", "x"), ("zl", "c")
    rows = P(shard + tensor, None)
    return jax.shard_map(
        per_device,
        mesh=fine,
        in_specs=(
            P(shard, tensor), P(None, shard, tensor), P(None, shard),
            rows, rows, rows, rows, P(shard + tensor),
        ),
        out_specs=(rows, rows),
        check_vma=False,
    )
```

```python
import jax
import jax.numpy as jnp
from jax import lax
from jax.experimental import pallas as pl
from jax.experimental.pallas import tpu as pltpu
from jax.sharding import Mesh, PartitionSpec as P

D = 768
VOCAB = 49152
TOK = 1024
SAMPLES = 262144
BLK = 128
NB = D // BLK
CHIPS = 64
HALF = BLK // 2
STEPS = 7

momentum_decay = 0.9
damping_root = 0.5
count_scale = 64.0

CHIP_AXES = ("y", "zh", "x", "zl")
f32 = jnp.float32
bf16 = jnp.bfloat16

BLOCKS = [(f, i, j) for f in range(3) for i in range(NB) for j in range(i, NB)]


def vmem():
    return pl.BlockSpec(memory_space=pltpu.VMEM)


def smem():
    return pl.BlockSpec(memory_space=pltpu.SMEM)


def params():
    return pltpu.CompilerParams(vmem_limit_bytes=60 * 1024 * 1024)


def nt_dot(a, b):
    return lax.dot_general(a, b, (((1,), (1,)), ((), ())), preferred_element_type=f32)


def nn_dot(a, b):
    return lax.dot_general(a, b, (((1,), (0,)), ((), ())), preferred_element_type=f32)


def split(x):
    hi = x.astype(bf16)
    return hi, (x - hi.astype(f32)).astype(bf16)


def histogram_kernel(info, ids_ref, out_ref):
    first = info[0] * 4
    width = 1024
    high_rows = lax.broadcasted_iota(jnp.int32, (16, width), 0) + first
    low_rows = lax.broadcasted_iota(jnp.int32, (BLK, width), 0)
    for k in range(2):
        total = jnp.zeros((16, BLK), f32)
        for part in range(8):
            ids = ids_ref[k : k + 1, part * width : (part + 1) * width]
            high = (high_rows == (ids >> 7)).astype(f32).astype(bf16)
            low = (low_rows == (ids & 127)).astype(f32).astype(bf16)
            total = total + nt_dot(high, low)
        out_ref[k] = total


def swap_halves(x):
    return pltpu.roll(x, HALF, 1)


def pair_up(x, lane):
    hi, lo = split(x)
    return jnp.where(lane < HALF, hi.astype(f32), lo.astype(f32))


def gram_kernel(info, hist_ref, own_ref, own_c_ref, other_ref, other_c_ref, count_ref, out_ref, x_ref):
    zl, core = info[0], info[1]
    places = [2 * zl + core, 2 * zl + 1 - core, 2 * (1 - zl) + core, 2 * (1 - zl) + 1 - core]
    on_diagonal = (
        lax.broadcasted_iota(jnp.int32, (HALF, BLK), 1)
        == lax.broadcasted_iota(jnp.int32, (HALF, BLK), 0) + core * HALF
    )
    exact = []
    for f in range(3):
        for place, ref in zip(places, (own_ref, own_c_ref, other_ref, other_c_ref)):
            x_ref[pl.ds(pl.multiple_of(place * 192, 192), 192), :] = ref[f]
        x = x_ref[...]
        left = jnp.concatenate(
            [x_ref[pl.ds(pl.multiple_of(i * BLK + core * HALF, HALF), HALF), :] for i in range(NB)], axis=0
        )
        row = 1 if f == 2 else 0
        weight = jnp.concatenate([hist_ref[row, h : h + 1, :] for h in range(4)], axis=1)
        hi, lo = split(left.astype(f32) * weight)
        gram = nt_dot(hi, x) + nt_dot(lo, x)
        for b, (g, i, j) in enumerate(BLOCKS):
            if g == f:
                block = gram[i * HALF : (i + 1) * HALF, j * BLK : (j + 1) * BLK]
                out_ref[b] = block.astype(bf16)
                if i == j:
                    exact.append(jnp.sum(jnp.where(on_diagonal, block, 0.0), axis=0, keepdims=True))
    tokens = jnp.sum(count_ref[...].astype(f32), keepdims=True).reshape(1, 1)
    lane = lax.broadcasted_iota(jnp.int32, (1, BLK), 1)
    exact.append(jnp.where(lane < HALF, tokens, 0.0))
    exact = jnp.concatenate(exact + [jnp.zeros((HALF - len(exact), BLK), f32)], axis=0)
    exact = exact + swap_halves(exact)
    lane = lax.broadcasted_iota(jnp.int32, (HALF, BLK), 1)
    out_ref[CHIPS - 1] = pair_up(exact, lane).astype(bf16)


def total_kernel(info, in_ref, out_ref):
    total = jnp.sum(in_ref[...].astype(f32), axis=0) * (1.0 / SAMPLES)
    lane = lax.broadcasted_iota(jnp.int32, (HALF, BLK), 1)
    exact = pair_up(total + swap_halves(total), lane)
    total = jnp.where(info[0] == CHIPS - 1, exact, total).astype(bf16)
    for s in range(CHIPS):
        out_ref[s] = total


def step(y, start, keep, scale, r_ref):
    hi, lo = split(y)
    return start + y * keep - scale * (nn_dot(hi, r_ref[...]) + nn_dot(lo, r_ref[...]))


def thin_step(y, start, keep, scale, r_ref):
    hi, lo = split(y)
    both = nn_dot(jnp.concatenate([hi, lo], axis=0), r_ref[...])
    return start + y * keep - scale * (both[:8] + both[8:])


def finish_kernel(
    info, own_ref, other_ref, p_ref, p_mom_ref, g_ref, e_mom_ref, count_ref,
    p_out_ref, e_out_ref, r_ref, y_ref,
):
    core, flat = info[0], info[1]
    row = lax.broadcasted_iota(jnp.int32, (HALF, BLK), 0)
    col = lax.broadcasted_iota(jnp.int32, (HALF, BLK), 1)
    squares = [jnp.zeros((HALF, BLK), f32) for _ in range(3)]
    for part, ref in ((core, own_ref), (1 - core, other_ref)):
        off_diagonal = col != row + part * HALF
        for b, (f, i, j) in enumerate(BLOCKS):
            start = pl.multiple_of(i * BLK + part * HALF, HALF)
            block = ref[b]
            wide = block.astype(f32)
            if i == j:
                wide = jnp.where(off_diagonal, wide, 0.0)
                block = wide.astype(bf16)
                squares[f] = squares[f] + wide * wide
            else:
                squares[f] = squares[f] + 2.0 * (wide * wide)
            r_ref[f, pl.ds(start, HALF), j * BLK : (j + 1) * BLK] = block
    for b, (f, i, j) in enumerate(BLOCKS):
        if i != j:
            block = r_ref[f, i * BLK : (i + 1) * BLK, j * BLK : (j + 1) * BLK]
            r_ref[f, j * BLK : (j + 1) * BLK, i * BLK : (i + 1) * BLK] = block.T

    own = own_ref[CHIPS - 1].astype(f32)
    other = other_ref[CHIPS - 1].astype(f32)
    own = own + swap_halves(own)
    other = other + swap_halves(other)
    exact = jnp.where((col < HALF) == (core == 0), own, other)
    tokens = (own + other)[18:19, 0:1] * float(SAMPLES)
    diagonals = [
        jnp.concatenate([exact[f * NB + i : f * NB + i + 1, :] for i in range(NB)], axis=1) for f in range(3)
    ]
    traces = [jnp.sum(d, keepdims=True) for d in diagonals]
    squares = [jnp.sum(s, keepdims=True) + jnp.sum(d * d, keepdims=True) for s, d in zip(squares, diagonals)]
    ratio = jnp.sqrt(traces[0] / traces[1])
    embed_ratio = jnp.sqrt(tokens / count_scale / VOCAB / (traces[2] / D))
    shifts = [damping_root * ratio, damping_root / ratio, damping_root / embed_ratio]
    scales, keeps = [], []
    for f in range(3):
        q = squares[f] + 2.0 * shifts[f] * traces[f] + D * shifts[f] * shifts[f]
        scales.append(1.0 / jnp.sqrt(q))
        keeps.append(1.0 - scales[f] * (diagonals[f] + shifts[f]))

    half = 192
    row = lax.broadcasted_iota(jnp.int32, (8, D), 0)
    col = lax.broadcasted_iota(jnp.int32, (8, D), 1)
    unit = jnp.where((row < 6) & (col == flat * 6 + row), 1.0, 0.0)

    def first(_, carry):
        a, y = carry
        a = thin_step(a, unit, keeps[0], scales[0], r_ref.at[0])
        y = step(y, g_ref[0:half, :], keeps[2], scales[2], r_ref.at[2])
        return a, y

    a, y = lax.fori_loop(0, STEPS, first, (unit, g_ref[0:half, :]))
    y_ref[0:half, :] = y
    a_hi, a_lo = split(a * scales[0])
    p_hi, p_lo = split(p_ref[...])
    mixed = nn_dot(a_hi, p_hi) + nn_dot(a_lo, p_hi) + nn_dot(a_hi, p_lo)

    def second(_, carry):
        a, y = carry
        a = thin_step(a, mixed, keeps[1], scales[1], r_ref.at[1])
        y = step(y, g_ref[half:, :], keeps[2], scales[2], r_ref.at[2])
        return a, y

    a, y = lax.fori_loop(0, STEPS, second, (mixed, g_ref[half:, :]))
    y_ref[half:, :] = y
    p_out_ref[...] = momentum_decay * p_mom_ref[...] + (a * scales[1])[0:6]
    row_scale = count_ref[...].astype(f32) / count_scale + damping_root * embed_ratio
    e_out_ref[...] = momentum_decay * e_mom_ref[...] + y_ref[...] * scales[2] / row_scale


def to_other(x, axis):
    return lax.ppermute(x, axis, [(0, 1), (1, 0)])


def exchange(x):
    return lax.all_to_all(x, CHIP_AXES, split_axis=0, concat_axis=0, tiled=True)


def per_device(acts, out_grads, sampled_rows, proj_grad, proj_momentum, embed_grad, embed_momentum, token_counts):
    zl, core = lax.axis_index("zl"), lax.axis_index("c")
    chip = lax.axis_index(CHIP_AXES)
    flat = chip * 2 + core

    features = jnp.concatenate([acts.T[None], jnp.transpose(out_grads, (0, 2, 1))], axis=0)
    keep = lax.dynamic_slice_in_dim(features, zl * 512, 512, 2)
    send = lax.dynamic_slice_in_dim(features, (1 - zl) * 512, 512, 2)
    send, keep, p_rows = lax.optimization_barrier((send, keep, proj_grad))
    other = to_other(send, "zl")
    keep_c = to_other(keep, "c")
    other_c = to_other(other, "c")

    hist = pl.pallas_call(
        histogram_kernel,
        out_shape=jax.ShapeDtypeStruct((2, 16, BLK), f32),
        in_specs=[smem(), vmem()],
        out_specs=vmem(),
        compiler_params=params(),
        name="histogram",
    )(jnp.stack([zl]), sampled_rows)

    parts = pl.pallas_call(
        gram_kernel,
        out_shape=jax.ShapeDtypeStruct((CHIPS, HALF, BLK), bf16),
        in_specs=[smem()] + [vmem()] * 6,
        out_specs=vmem(),
        scratch_shapes=[pltpu.VMEM((D, 512), bf16)],
        compiler_params=params(),
        name="gram",
    )(jnp.stack([zl, core]), hist, keep, keep_c, other, other_c, token_counts.reshape(3, BLK))

    p_own = exchange(jnp.broadcast_to(p_rows[None], (CHIPS,) + proj_grad.shape))
    arrived = exchange(parts)
    p_other = to_other(p_own, "c")
    p_pair = jnp.stack([jnp.where(core == 0, p_own, p_other), jnp.where(core == 0, p_other, p_own)], axis=1)
    p_full = p_pair.reshape(D, D)

    spread = pl.pallas_call(
        total_kernel,
        out_shape=jax.ShapeDtypeStruct((CHIPS, HALF, BLK), bf16),
        in_specs=[smem(), vmem()],
        out_specs=vmem(),
        compiler_params=params(),
        name="total",
    )(jnp.stack([chip]), arrived)
    own_blocks = exchange(spread)
    other_blocks = to_other(own_blocks, "c")

    return pl.pallas_call(
        finish_kernel,
        out_shape=(
            jax.ShapeDtypeStruct(proj_momentum.shape, f32),
            jax.ShapeDtypeStruct(embed_momentum.shape, f32),
        ),
        in_specs=[smem()] + [vmem()] * 7,
        out_specs=(vmem(), vmem()),
        scratch_shapes=[
            pltpu.VMEM((3, D, D), bf16),
            pltpu.VMEM((384, D), f32),
        ],
        compiler_params=params(),
        name="finish",
    )(
        jnp.stack([core, flat]), own_blocks, other_blocks, p_full, proj_momentum, embed_grad, embed_momentum,
        token_counts.reshape(-1, 1),
    )


def solution(mesh):
    fine = Mesh(mesh.devices.reshape(4, 2, 4, 2, 2), ("y", "zh", "x", "zl", "c"))
    shard, tensor = ("y", "zh", "x"), ("zl", "c")
    rows = P(shard + tensor, None)
    return jax.shard_map(
        per_device,
        mesh=fine,
        in_specs=(
            P(shard, tensor), P(None, shard, tensor), P(None, shard),
            rows, rows, rows, rows, P(shard + tensor),
        ),
        out_specs=(rows, rows),
        check_vma=False,
    )
```
